512 devices in a mesh: req: 32 (over x, z), tp: 16 (over y, core).
Axes of the slice: x: 4, y: 8, z: 8, core: 2. Of those that a mesh axis runs over, the one named last changes fastest.
Arguments:
- hidden: bfloat16 [32768, 2048], P(('req', 'tp')), may hold values from -6 to 6
- ln_gain: float32 [2048], replicated, may hold values from 0.1 to 1.9
- w_qkv: bfloat16 [2048, 3, 2048], P(None, None, 'tp'), may hold values from -0.125 to 0.125
- w_out: bfloat16 [2048, 2048], P('tp'), may hold values from -0.125 to 0.125
- cache_kv: bfloat16 [2, 512, 256, 2048], P(None, 'req', None, 'tp'), may hold values from -6 to 6
- cache_len: int32 [512], P('req'), may hold values from 16 to 256, as said below
- ancestors: int32 [512, 64, 64], P('req'), may hold values from 0 to 1, as said below
- accepted: int32 [512, 8], P('req'), may hold values from 0 to 14, as said below
Outputs:
- attn_proj: bfloat16 [32768, 2048], P(('req', 'tp'))
- kept_kv: bfloat16 [2, 512, 8, 2048], P(None, 'req', None, 'tp')
The draws below stay inside these ranges and needn't reach their ends.
Inputs may be any that keep to these rules, and one draw needn't show every extreme that they name: `cache_len`: at least one request of the whole batch has exactly 256 cached positions. `ancestors`: entry (r, i, j) is 1 exactly where draft token j is token i or an ancestor of it in request r's tree; a token's parent has a lower index and token 0 is the root. `accepted`: each row holds, in increasing order, the first 8 tokens of a path down from the root of the request's tree, each entry the parent of the next.
All inputs are finite; a program needn't handle non-finite values.
Results may differ from the reference program's by a relative error of at most 0.018.
Values may be sent and summed in bfloat16 or wider, within the bound.
A program may use at most 64 MiB of HBM per device.

```python
import math
import jax
import jax.numpy as jnp
from jax import lax

D = 2048
H = 16
HD = 128
REQ_DEV = 16
DRAFT = 64
ACC = 8
CMAX = 256
REQS = 512
TOKENS = 32768
N_TP = 16


def build_trees(key):
    tree_key = jax.random.fold_in(key, 11)
    pick_key = jax.random.fold_in(key, 31)
    steps_back = jax.random.randint(tree_key, (REQS, DRAFT), 1, 3)
    chosen_request = jax.random.randint(pick_key, (), 0, REQS)
    request_ids = jnp.arange(REQS)
    steps_back = jnp.where(request_ids[:, None] == chosen_request, 2, steps_back)
    indices = jnp.arange(DRAFT)
    parent = jnp.maximum(indices[None, :] - steps_back, 0)

    def grow(node, masks):
        onehot = (parent[:, node][:, None] == indices[None, :]).astype(jnp.int32)
        row = jnp.sum(onehot[:, :, None] * masks, axis=1)
        row = jnp.where(indices[None, :] == node, 1, row)
        return lax.dynamic_update_slice_in_dim(masks, row[:, None, :], node, 1)
    masks = lax.fori_loop(0, DRAFT, grow, jnp.zeros((REQS, DRAFT, DRAFT), jnp.int32))
    end_key = jax.random.fold_in(key, 23)
    ends = jax.random.randint(end_key, (REQS,), DRAFT // 2, DRAFT)
    ends = jnp.where(request_ids == chosen_request, DRAFT - 2, ends)
    chosen = (ends[:, None] == indices[None, :]).astype(jnp.int32)
    path = jnp.sum(chosen[:, :, None] * masks, axis=1)
    rank = jnp.cumsum(path, axis=1) - 1
    slots = jnp.arange(ACC)
    hits = path[:, None, :] * (rank[:, None, :] == slots[None, :, None]).astype(jnp.int32)
    accepted = jnp.sum(hits * indices[None, None, :], axis=2)
    return (masks, accepted.astype(jnp.int32))


def draw_ancestors(key, part):
    masks, accepted = build_trees(key)
    return masks


def draw_accepted(key, part):
    masks, accepted = build_trees(key)
    return accepted


def draw_cache_len(key, part):
    level_key = jax.random.fold_in(key, 7)
    jitter_key = jax.random.fold_in(key, 9)
    pick_key = jax.random.fold_in(key, 8)
    groups = REQS // REQ_DEV
    levels = jax.random.randint(level_key, (groups,), CMAX // 8, CMAX + 1)
    per_request = jnp.repeat(levels, REQ_DEV)
    jitter = jax.random.randint(jitter_key, (REQS,), 0, per_request // 4 + 1)
    lengths = per_request - jitter
    pick = jax.random.randint(pick_key, (), 0, REQS)
    return jnp.where(jnp.arange(REQS) == pick, CMAX, lengths).astype(jnp.int32)


def shard_levels(stream_key, extent, pieces, low, largest):
    factor_of = 1.0
    for axis_at, shards_of in pieces:
        draws = jax.random.uniform(jax.random.fold_in(jax.random.fold_in(stream_key, 6), axis_at), (shards_of,), jnp.float32, low / len(pieces), largest / len(pieces))
        factor_of = factor_of * jnp.repeat(jnp.exp(draws), extent[axis_at] // shards_of).reshape((-1,) + (1,) * (len(extent) - 1 - axis_at))
    return factor_of


def gaussian(key, dims, width, most, shards=(), held_as=jnp.bfloat16):
    factor_of = shard_levels(key, dims, shards, -0.22, 0.18) if shards else 1.0
    array = jax.random.normal(key, dims, jnp.float32) * width * factor_of
    return jnp.minimum(jnp.maximum(array, -most), most).astype(held_as)


def setup_inputs(seed: int = 0) -> dict:
    key_of = jax.random.split(jax.random.key(seed), 9)
    return {
        "hidden": gaussian(key_of[0], (TOKENS, D), 1.0, 6.0, ((0, 512),)),
        "ln_gain": jnp.clip(1.0 + 0.18 * jax.random.normal(key_of[1], (D,), jnp.float32), 0.1, 1.9),
        "w_qkv": gaussian(key_of[2], (D, 3, H * HD), D ** -0.5, 0.125, ((2, 16),)),
        "w_out": gaussian(key_of[3], (H * HD, D), (H * HD) ** -0.5, 0.125, ((0, 16),)),
        "cache_kv": gaussian(key_of[4], (2, REQS, CMAX, H * HD), 1.0, 6.0, ((1, 32), (3, 16))),
        "cache_len": draw_cache_len(jax.random.fold_in(key_of[8], 71), 0),
        "ancestors": draw_ancestors(jax.random.fold_in(key_of[8], 71), 0),
        "accepted": draw_accepted(jax.random.fold_in(key_of[8], 71), 0),
    }


def one_request(items):
    queries, new_keys, new_values, cache_keys, cache_values, length, mask, depth = items
    scale = 1.0 / math.sqrt(HD)
    slopes = jnp.exp2(-8.0 * (jnp.arange(H).astype(jnp.float32) + 1.0) / H)
    qf = queries.astype(jnp.float32)
    cells = jnp.arange(CMAX)
    cache_scores = jnp.einsum('ihd,jhd->hij', qf, cache_keys.astype(jnp.float32)) * scale + slopes[:, None, None] * cells.astype(jnp.float32)[None, None, :]
    draft_pos = (length + depth).astype(jnp.float32)
    draft_scores = jnp.einsum('ihd,jhd->hij', qf, new_keys.astype(jnp.float32)) * scale + slopes[:, None, None] * draft_pos[None, None, :]
    scores = jnp.concatenate([cache_scores, draft_scores], axis=2)
    valid_cache = jnp.broadcast_to((cells < length)[None, :], (DRAFT, CMAX))
    valid = jnp.concatenate([valid_cache, mask == 1], axis=1)[None, :, :]
    scores = jnp.where(valid, scores, -1e+30)
    top = lax.optimization_barrier(jnp.max(scores, axis=2, keepdims=True))
    expo = jnp.where(valid, jnp.exp(scores - top), 0.0)
    total = lax.optimization_barrier(jnp.sum(expo, axis=2))
    weights = expo.astype(jnp.bfloat16).astype(jnp.float32)
    values_all = jnp.concatenate([cache_values, new_values], axis=0).astype(jnp.float32)
    summed = jnp.einsum('hij,jhd->ihd', weights, values_all)
    return (summed / jnp.transpose(total)[:, :, None]).astype(jnp.bfloat16)

def reference(hidden, ln_gain, w_qkv, w_out, cache_kv, cache_len, ancestors, accepted):
    values = hidden.astype(jnp.float32)
    mean = lax.optimization_barrier(jnp.mean(values, axis=1, keepdims=True))
    centered = values - mean
    var = lax.optimization_barrier(jnp.mean(centered * centered, axis=1, keepdims=True))
    normed = (centered * lax.rsqrt(var + 1e-05) * ln_gain[None, :]).astype(jnp.bfloat16)
    joined = jnp.dot(normed, w_qkv.reshape(D, 3 * H * HD), preferred_element_type=jnp.float32).astype(jnp.bfloat16)
    joined = joined.reshape(REQS, DRAFT, 3, H, HD)
    queries = joined[:, :, 0]
    new_keys = joined[:, :, 1]
    new_values = joined[:, :, 2]
    depth = lax.optimization_barrier(jnp.sum(ancestors, axis=2)) - 1
    cache_keys = cache_kv[0].reshape(REQS, CMAX, H, HD)
    cache_values = cache_kv[1].reshape(REQS, CMAX, H, HD)
    attn = lax.map(one_request, (queries, new_keys, new_values, cache_keys, cache_values, cache_len, ancestors, depth))
    attn = attn.reshape(TOKENS, H * HD)
    group = H * HD // N_TP
    summed = jnp.zeros((TOKENS, D), jnp.float32)
    for index in range(N_TP):
        part = jnp.dot(attn[:, index * group:(index + 1) * group], w_out[index * group:(index + 1) * group], preferred_element_type=jnp.float32).astype(jnp.bfloat16)
        part = lax.optimization_barrier(part)
        summed = summed + part.astype(jnp.float32)
    attn_proj = summed.astype(jnp.bfloat16)
    onehot = (accepted[:, :, None] == jnp.arange(DRAFT)[None, None, :]).astype(jnp.float32)
    kept_keys = jnp.einsum('rad,rdc->rac', onehot, new_keys.reshape(REQS, DRAFT, H * HD).astype(jnp.float32))
    kept_values = jnp.einsum('rad,rdc->rac', onehot, new_values.reshape(REQS, DRAFT, H * HD).astype(jnp.float32))
    kept_kv = jnp.stack([kept_keys, kept_values]).astype(jnp.bfloat16)
    return (attn_proj, kept_kv)
```

```python
import functools
import math

import jax
import jax.numpy as jnp
from jax import lax
from jax.experimental import pallas as pl
from jax.experimental.pallas import tpu as pltpu
from jax.sharding import PartitionSpec as P

HD = 128
CORES = 2
MESH = pl.DeviceIdType.MESH


class Ring:
    def __init__(self, n, me, device, slot, send, recv):
        self.n, self.me, self.device, self.slot = n, me, device, slot
        self.send, self.recv = send, recv
        self.far = n // 2
        self.sent = []

    def live(self, way, dist, h):
        return dist < self.far or (dist == self.far and h == way)

    def place(self, way, dist):
        step = self.n - dist if way == 0 else dist
        return lax.rem(self.me + step, self.n)

    def copy(self, way, dist, h):
        owner = self.me if dist == 1 else self.place(way, dist - 1)
        to = lax.rem(self.me + (1 if way == 0 else self.n - 1), self.n)
        ref = self.slot(owner, h)
        return pltpu.make_async_remote_copy(
            src_ref=ref,
            dst_ref=ref,
            send_sem=self.send.at[way, dist - 1, h],
            recv_sem=self.recv.at[way, dist - 1, h],
            device_id=self.device(to),
            device_id_type=MESH,
        )

    def start(self, way, dist, h):
        if self.live(way, dist, h):
            copy = self.copy(way, dist, h)
            copy.start()
            self.sent.append(copy)

    def own(self):
        for h in range(2):
            for way in range(2):
                self.start(way, 1, h)

    def step(self, dist, h, then=None):
        for way in range(2):
            if self.live(way, dist, h):
                ref = self.slot(self.place(way, dist), h)
                pltpu.make_async_remote_copy(
                    src_ref=ref,
                    dst_ref=ref,
                    send_sem=self.send.at[way, dist - 1, h],
                    recv_sem=self.recv.at[way, dist - 1, h],
                    device_id=self.device(lax.rem(self.me + 1, self.n)),
                    device_id_type=MESH,
                ).wait_recv()
                self.start(way, dist + 1, h)
                if then is not None:
                    then(way, dist, h)

    def events(self):
        return [(d, h) for d in range(1, self.far) for h in range(2)] + [(self.far, None)]

    def event(self, event, then=None):
        dist, h = event
        for half in (0, 1) if h is None else (h,):
            self.step(dist, half, then)

    def drain(self):
        for copy in self.sent:
            copy.wait_send()


def kernel(
    nx, nz, ny,
    hidden, gain, w_out, lens, accepted, w_qkv, cache, ancestors,
    out, kept,
    nbuf, wbuf, wq, kv, anc, asend, arecv, obuf, acc,
    local_sem, w_send, w_recv,
    y_send, y_recv, p_send, p_recv,
    xa_send, xa_recv, za_send, za_recv, zb_send, zb_recv, xb_send, xb_recv,
    a_send, a_recv, r_send, r_recv, o_send, o_recv,
):
    req, tp = lax.axis_index("req"), lax.axis_index("tp")
    x, z = lax.div(req, nz), lax.rem(req, nz)
    y, core = lax.div(tp, CORES), lax.rem(tp, CORES)
    ntp = ny * CORES
    half_heads = ntp // 2
    quarter = ntp // 4
    mate = (req, y * CORES + (1 - core))
    drafts, width = hidden.shape
    half_rows = drafts // 2
    half_width = width // CORES
    piece_rows, piece_cols = HD // nz, half_width // nx

    barrier = pltpu.get_barrier_semaphore()
    x_dev = lambda pos: (pos * nz + z, tp)
    z_dev = lambda pos: (x * nz + pos, tp)
    y_dev = lambda pos: (req, pos * CORES + core)
    peers = [(req, lax.rem(tp + o, ntp)) for o in range(1, ntp)]
    peers += [x_dev(lax.rem(x + s, nx)) for s in (1, nx - 1)]
    peers += [z_dev(lax.rem(z + s, nz)) for s in (1, nz - 1)]
    for peer in peers:
        pl.semaphore_signal(barrier, inc=1, device_id=peer, device_id_type=MESH)

    loads = [pltpu.make_async_copy(w_qkv.at[i], wq.at[:, pl.ds(i * HD, HD)], local_sem.at[i]) for i in range(3)]
    loads.append(pltpu.make_async_copy(cache, kv, local_sem.at[3]))
    loads.append(pltpu.make_async_copy(ancestors, anc, local_sem.at[4]))
    for load in loads:
        load.start()

    rows = hidden[...].astype(jnp.float32)
    mean = jnp.mean(rows, axis=1, keepdims=True)
    centered = rows - mean
    var = jnp.mean(centered * centered, axis=1, keepdims=True)
    normed = (centered * lax.rsqrt(var + 1e-05) * gain[...]).astype(jnp.bfloat16)
    nbuf[y, core, 0] = normed[:half_rows]
    nbuf[y, core, 1] = normed[half_rows:]

    pl.semaphore_wait(barrier, len(peers))

    def piece(c):
        return w_out.at[
            pl.ds(pl.multiple_of(z * piece_rows, piece_rows), piece_rows),
            pl.ds(pl.multiple_of(c * half_width + x * piece_cols, piece_cols), piece_cols),
        ]

    sends = []
    for o in range(1, ntp):
        to = lax.rem(tp + o, ntp)
        sends.append(pltpu.make_async_remote_copy(
            src_ref=piece(lax.rem(to, CORES)),
            dst_ref=wbuf.at[x, z, tp],
            send_sem=w_send.at[o],
            recv_sem=w_recv.at[o],
            device_id=(req, to),
            device_id_type=MESH,
        ))
        sends[-1].start()
    own_piece = pltpu.make_async_copy(piece(core), wbuf.at[x, z, tp], local_sem.at[5])
    own_piece.start()

    ring_y = Ring(ny, y, y_dev, lambda pos, h: nbuf.at[pos, core, h], y_send, y_recv)
    ring_y.own()

    def share(way, dist, h):
        owner = ring_y.place(way, dist) if dist else y
        copy = pltpu.make_async_remote_copy(
            src_ref=nbuf.at[owner, core, h],
            dst_ref=nbuf.at[owner, core, h],
            send_sem=p_send.at[way, dist, h],
            recv_sem=p_recv.at[way, dist, h],
            device_id=mate,
            device_id_type=MESH,
        )
        copy.start()
        sends.append(copy)

    def shared(way, dist, h):
        owner = ring_y.place(way, dist) if dist else y
        ref = nbuf.at[owner, 1 - core, h]
        pltpu.make_async_remote_copy(
            src_ref=ref, dst_ref=ref,
            send_sem=p_send.at[way, dist, h], recv_sem=p_recv.at[way, dist, h],
            device_id=mate, device_id_type=MESH,
        ).wait_recv()

    for h in range(2):
        share(0, 0, h)

    slope = jnp.exp2(jnp.full((1, HD), -8.0 / ntp, jnp.float32) * (tp + 1).astype(jnp.float32))[:, :1]
    scale = 1.0 / math.sqrt(HD)
    contract_last = (((1,), (1,)), ((), ()))

    def request(rid, q, k, v):
        length = lens[rid]
        mask = anc[rid]
        cells = kv.shape[2]
        depth = lax.dot_general(
            jnp.ones((8, drafts), jnp.bfloat16), mask.astype(jnp.float32).astype(jnp.bfloat16),
            contract_last, preferred_element_type=jnp.float32,
        )[:1] - 1.0
        cell = lax.broadcasted_iota(jnp.int32, (1, cells), 1)
        s_cache = lax.dot_general(q, kv[0, rid], contract_last, preferred_element_type=jnp.float32)
        s_cache = s_cache * scale + slope * cell.astype(jnp.float32)
        s_cache = jnp.where(cell < length, s_cache, -1e30)
        s_draft = lax.dot_general(q, k, contract_last, preferred_element_type=jnp.float32)
        s_draft = s_draft * scale + slope * (length.astype(jnp.float32) + depth)
        s_draft = jnp.where(mask == 1, s_draft, -1e30)
        top = jnp.maximum(jnp.max(s_cache, axis=1, keepdims=True), jnp.max(s_draft, axis=1, keepdims=True))
        e_cache = jnp.exp(s_cache - top)
        e_draft = jnp.exp(s_draft - top)
        total = jnp.sum(e_cache, axis=1, keepdims=True) + jnp.sum(e_draft, axis=1, keepdims=True)
        summed = jnp.dot(e_cache.astype(jnp.bfloat16), kv[1, rid], preferred_element_type=jnp.float32)
        summed += jnp.dot(e_draft.astype(jnp.bfloat16), v, preferred_element_type=jnp.float32)
        slots = kept.shape[2]
        slot = lax.broadcasted_iota(jnp.int32, (slots, drafts), 0)
        chosen = jnp.zeros((slots, drafts), jnp.int32)
        for a in range(slots):
            chosen = jnp.where(slot == a, accepted[a, rid], chosen)
        onehot = jnp.where(chosen == lax.broadcasted_iota(jnp.int32, (slots, drafts), 1), 1.0, 0.0).astype(jnp.bfloat16)
        kept[0, rid] = jnp.dot(onehot, k, preferred_element_type=jnp.float32).astype(jnp.bfloat16)
        kept[1, rid] = jnp.dot(onehot, v, preferred_element_type=jnp.float32).astype(jnp.bfloat16)
        return (summed / total).astype(jnp.bfloat16)

    order = []

    def attend(way, dist):
        if dist == 0:
            waits = [(0, 0, 0), (0, 0, 1)]
        elif dist < ring_y.far:
            waits = [(way, dist, 0), (way, dist, 1)]
        else:
            waits = [(0, dist, 0), (1, dist, 1)]
        for w in waits:
            shared(*w)
        owner = ring_y.place(way, dist) if dist else y
        tokens = nbuf[owner].reshape(CORES * drafts, width)
        joined = jnp.dot(tokens, wq[...], preferred_element_type=jnp.float32).astype(jnp.bfloat16)
        result = []
        for r in range(CORES):
            part = joined[r * drafts:(r + 1) * drafts]
            result.append(request(owner * CORES + r, part[:, :HD], part[:, HD:2 * HD], part[:, 2 * HD:]))
        result = jnp.concatenate(result, axis=0)
        if dist == 0:
            arecv[y, core] = result
            relay(0)
        else:
            offset = ny - dist if way == 0 else dist
            asend[offset] = result
            copy = pltpu.make_async_remote_copy(
                src_ref=asend.at[offset], dst_ref=arecv.at[y, core],
                send_sem=a_send.at[offset], recv_sem=a_recv.at[offset],
                device_id=y_dev(owner), device_id_type=MESH,
            )
            copy.start()
            sends.append(copy)
            order.append(offset)

    def source(offset):
        return lax.rem(y + ny - offset, ny) if offset else y

    def relay(offset):
        ref = arecv.at[source(offset), core]
        copy = pltpu.make_async_remote_copy(
            src_ref=ref, dst_ref=ref,
            send_sem=r_send.at[offset], recv_sem=r_recv.at[offset],
            device_id=mate, device_id_type=MESH,
        )
        copy.start()
        sends.append(copy)

    ring_xa = Ring(nx, x, x_dev, lambda pos, h: wbuf.at[pos, z, pl.ds(h * quarter, quarter)], xa_send, xa_recv)
    ring_za = Ring(nz, z, z_dev, lambda pos, h: wbuf.at[pl.ds(h * (nx // 2), nx // 2), pos, pl.ds(0, half_heads)], za_send, za_recv)
    ring_zb = Ring(nz, z, z_dev, lambda pos, h: wbuf.at[x, pos, pl.ds(half_heads + h * quarter, quarter)], zb_send, zb_recv)
    ring_xb = Ring(nx, x, x_dev, lambda pos, h: wbuf.at[pos, pl.ds(h * (nz // 2), nz // 2), pl.ds(half_heads, half_heads)], xb_send, xb_recv)

    own_piece.wait()
    for o in range(1, ntp):
        ref = wbuf.at[x, z, lax.rem(tp + ntp - o, ntp)]
        pltpu.make_async_remote_copy(
            src_ref=ref, dst_ref=ref, send_sem=w_send.at[o], recv_sem=w_recv.at[o],
            device_id=mate, device_id_type=MESH,
        ).wait_recv()
    ring_xa.own()
    ring_zb.own()
    for load in loads:
        load.wait()
    attend(0, 0)

    first = ring_zb.events()
    second_a = ring_za.events()
    second_b = ring_xb.events()
    pending = []
    for event in ring_xa.events():
        ring_xa.event(event)
    ring_za.own()
    for i, event in enumerate(ring_y.events()):
        ring_y.event(event, share)
        for _ in range(2):
            if first:
                ring_zb.event(first.pop(0))
                if not first:
                    ring_xb.own()
        if i and second_a:
            ring_za.event(second_a.pop(0))
        if not first and i >= 4 and second_b:
            ring_xb.event(second_b.pop(0))
        dist, h = event
        if h == 1:
            pending += [(0, dist), (1, dist)]
        elif h is None:
            pending.insert(0, (0, dist))
        if pending:
            attend(*pending.pop(0))
    while first:
        ring_zb.event(first.pop(0))
        if not first:
            ring_xb.own()
    while pending or second_a or second_b:
        if second_a:
            ring_za.event(second_a.pop(0))
        if second_b:
            ring_xb.event(second_b.pop(0))
        if pending:
            attend(*pending.pop(0))

    for offset in order:
        ref = arecv.at[source(offset), core]
        pltpu.make_async_remote_copy(
            src_ref=ref, dst_ref=ref, send_sem=a_send.at[offset], recv_sem=a_recv.at[offset],
            device_id=mate, device_id_type=MESH,
        ).wait_recv()
        relay(offset)

    for n, offset in enumerate([0] + order):
        chip = source(offset)
        ref = arecv.at[chip, 1 - core]
        pltpu.make_async_remote_copy(
            src_ref=ref, dst_ref=ref, send_sem=r_send.at[offset], recv_sem=r_recv.at[offset],
            device_id=mate, device_id_type=MESH,
        ).wait_recv()
        left = jnp.concatenate([arecv[chip, c] for c in range(CORES)], axis=1)
        for b in range(nx):
            right = jnp.concatenate(
                [wbuf[b, :, chip * CORES + c].reshape(HD, piece_cols) for c in range(CORES)], axis=0
            )
            columns = pl.ds(b * piece_cols, piece_cols)
            term = jnp.dot(left, right, preferred_element_type=jnp.float32)
            acc[:, columns] = term if n == 0 else acc[:, columns] + term

    for c in range(CORES):
        asend_rows = acc[c * drafts:(c + 1) * drafts].astype(jnp.bfloat16)
        obuf[c] = asend_rows
    last = pltpu.make_async_remote_copy(
        src_ref=obuf.at[1 - core], dst_ref=obuf.at[2], send_sem=o_send, recv_sem=o_recv,
        device_id=mate, device_id_type=MESH,
    )
    last.start()
    mine = pl.ds(pl.multiple_of(core * half_width, half_width), half_width)
    other = pl.ds(pl.multiple_of((1 - core) * half_width, half_width), half_width)
    out[:, mine] = obuf[core]
    last.wait()
    out[:, other] = obuf[2]
    for copy in sends:
        copy.wait_send()
    for ring in (ring_y, ring_xa, ring_za, ring_zb, ring_xb):
        ring.drain()


def on_device(nz, req_size, tp_size, hidden, ln_gain, w_qkv, w_out, cache_kv, cache_len, ancestors, accepted):
    nx, ny = req_size // nz, tp_size // CORES
    drafts, width = hidden.shape
    requests, slots = accepted.shape
    half_width = width // CORES
    bf16 = jnp.bfloat16
    dma = pltpu.SemaphoreType.DMA
    vmem = pl.BlockSpec(memory_space=pltpu.VMEM)
    smem = pl.BlockSpec(memory_space=pltpu.SMEM)
    hbm = pl.BlockSpec(memory_space=pl.ANY)
    ring = lambda n: [dma((2, n // 2, 2))] * 2
    out, kept = pl.pallas_call(
        functools.partial(kernel, nx, nz, ny),
        out_shape=(
            jax.ShapeDtypeStruct((drafts, width), bf16),
            jax.ShapeDtypeStruct((2, requests, slots, HD), bf16),
        ),
        in_specs=[vmem, vmem, vmem, smem, smem, hbm, hbm, hbm],
        out_specs=(vmem, vmem),
        scratch_shapes=[
            pltpu.VMEM((ny, CORES, 2, drafts // 2, width), bf16),
            pltpu.VMEM((nx, nz, tp_size, HD // nz, half_width // nx), bf16),
            pltpu.VMEM((width, 3 * HD), bf16),
            pltpu.VMEM(cache_kv.shape, bf16),
            pltpu.VMEM(ancestors.shape, jnp.int32),
            pltpu.VMEM((ny, CORES * drafts, HD), bf16),
            pltpu.VMEM((ny, CORES, CORES * drafts, HD), bf16),
            pltpu.VMEM((3, drafts, half_width), bf16),
            pltpu.VMEM((CORES * drafts, half_width), jnp.float32),
            dma((6,)),
            dma((tp_size,)),
            dma((tp_size,)),
            *ring(ny),
            dma((2, ny // 2 + 1, 2)),
            dma((2, ny // 2 + 1, 2)),
            *ring(nx), *ring(nz), *ring(nz), *ring(nx),
            dma((ny,)), dma((ny,)), dma((ny,)), dma((ny,)),
            dma, dma,
        ],
        compiler_params=pltpu.CompilerParams(
            collective_id=0, has_side_effects=True, vmem_limit_bytes=40 * 1024 * 1024
        ),
    )(
        hidden, ln_gain.reshape(1, width), w_out, cache_len, accepted.T,
        jnp.transpose(w_qkv, (1, 0, 2)), cache_kv, ancestors,
    )
    return (out, kept)


def solution(mesh, nz=8):
    placed = (
        P(("req", "tp"), None),
        P(),
        P(None, None, "tp"),
        P("tp", None),
        P(None, "req", None, "tp"),
        P("req"),
        P("req", None, None),
        P("req", None),
    )
    return jax.shard_map(
        functools.partial(on_device, nz, mesh.shape["req"], mesh.shape["tp"]),
        mesh=mesh,
        in_specs=placed,
        out_specs=(P(("req", "tp"), None), P(None, "req", None, "tp")),
        check_vma=False,
    )
```

```python
import functools
import math

import jax
import jax.numpy as jnp
from jax import lax
from jax.experimental import pallas as pl
from jax.experimental.pallas import tpu as pltpu
from jax.sharding import PartitionSpec as P

HD = 128
CORES = 2
MESH = pl.DeviceIdType.MESH


class Ring:
    def __init__(self, n, me, device, slot, send, recv):
        self.n, self.me, self.device, self.slot = n, me, device, slot
        self.send, self.recv = send, recv
        self.far = n // 2
        self.sent = []

    def live(self, way, dist, h):
        return dist < self.far or (dist == self.far and h == way)

    def place(self, way, dist):
        step = self.n - dist if way == 0 else dist
        return lax.rem(self.me + step, self.n)

    def copy(self, way, dist, h):
        owner = self.me if dist == 1 else self.place(way, dist - 1)
        to = lax.rem(self.me + (1 if way == 0 else self.n - 1), self.n)
        ref = self.slot(owner, h)
        return pltpu.make_async_remote_copy(
            src_ref=ref,
            dst_ref=ref,
            send_sem=self.send.at[way, dist - 1, h],
            recv_sem=self.recv.at[way, dist - 1, h],
            device_id=self.device(to),
            device_id_type=MESH,
        )

    def start(self, way, dist, h):
        if self.live(way, dist, h):
            copy = self.copy(way, dist, h)
            copy.start()
            self.sent.append(copy)

    def own(self):
        for h in range(2):
            for way in range(2):
                self.start(way, 1, h)

    def step(self, dist, h, then=None):
        for way in range(2):
            if self.live(way, dist, h):
                ref = self.slot(self.place(way, dist), h)
                pltpu.make_async_remote_copy(
                    src_ref=ref,
                    dst_ref=ref,
                    send_sem=self.send.at[way, dist - 1, h],
                    recv_sem=self.recv.at[way, dist - 1, h],
                    device_id=self.device(lax.rem(self.me + 1, self.n)),
                    device_id_type=MESH,
                ).wait_recv()
                self.start(way, dist + 1, h)
                if then is not None:
                    then(way, dist, h)

    def events(self):
        return [(d, h) for d in range(1, self.far) for h in range(2)] + [(self.far, None)]

    def event(self, event, then=None):
        dist, h = event
        for half in (0, 1) if h is None else (h,):
            self.step(dist, half, then)

    def drain(self):
        for copy in self.sent:
            copy.wait_send()


def kernel(
    nx, nz, ny,
    hidden_hbm, gain_hbm, w_out_hbm, lens_hbm, accepted_hbm, w_qkv, cache, ancestors,
    out, kept,
    hidden, gain, w_out, lens, accepted, nbuf, wlow, whigh, wq, kv, anc, asend, arecv, obuf, acc,
    local_sem, w_send, w_recv,
    y_send, y_recv, p_send, p_recv,
    z_send, z_recv, x_send, x_recv,
    a_send, a_recv, r_send, r_recv, o_send, o_recv,
):
    req, tp = lax.axis_index("req"), lax.axis_index("tp")
    x, z = lax.div(req, nz), lax.rem(req, nz)
    y, core = lax.div(tp, CORES), lax.rem(tp, CORES)
    ntp = ny * CORES
    half_heads = ntp // 2
    quarter = ntp // 4
    mate = (req, y * CORES + (1 - core))
    drafts, width = hidden.shape
    half_rows = drafts // 2
    half_width = width // CORES
    piece_rows, piece_cols = HD // nz, half_width // nx

    barrier = pltpu.get_barrier_semaphore()
    x_dev = lambda pos: (pos * nz + z, tp)
    z_dev = lambda pos: (x * nz + pos, tp)
    y_dev = lambda pos: (req, pos * CORES + core)
    peers = [(req, lax.rem(tp + o, ntp)) for o in range(1, ntp)]
    peers += [x_dev(lax.rem(x + s, nx)) for s in (1, nx - 1)]
    peers += [z_dev(lax.rem(z + s, nz)) for s in (1, nz - 1)]
    early = [
        pltpu.make_async_copy(src, dst, local_sem.at[6 + i])
        for i, (src, dst) in enumerate(((hidden_hbm, hidden), (gain_hbm, gain), (w_out_hbm, w_out)))
    ]
    for load in early:
        load.start()
    for peer in peers:
        pl.semaphore_signal(barrier, inc=1, device_id=peer, device_id_type=MESH)

    loads = [pltpu.make_async_copy(w_qkv.at[i], wq.at[:, pl.ds(i * HD, HD)], local_sem.at[i]) for i in range(3)]
    loads.append(pltpu.make_async_copy(cache, kv, local_sem.at[3]))
    loads.append(pltpu.make_async_copy(ancestors, anc, local_sem.at[4]))
    loads.append(pltpu.make_async_copy(lens_hbm, lens, local_sem.at[9]))
    loads.append(pltpu.make_async_copy(accepted_hbm, accepted, local_sem.at[10]))
    for load in loads:
        load.start()

    early[0].wait()
    early[1].wait()
    rows = hidden[...].astype(jnp.float32)
    mean = jnp.mean(rows, axis=1, keepdims=True)
    centered = rows - mean
    var = jnp.mean(centered * centered, axis=1, keepdims=True)
    normed = (centered * lax.rsqrt(var + 1e-05) * gain[...]).astype(jnp.bfloat16)
    nbuf[y, core, 0] = normed[:half_rows]
    nbuf[y, core, 1] = normed[half_rows:]

    early[2].wait()
    pl.semaphore_wait(barrier, len(peers))

    def low_piece(c):
        return w_out.at[
            pl.ds(pl.multiple_of(z * piece_rows, piece_rows), piece_rows),
            pl.ds(pl.multiple_of(c * half_width, half_width), half_width),
        ]

    def high_piece(c):
        return w_out.at[:, pl.ds(pl.multiple_of(c * half_width + x * piece_cols, piece_cols), piece_cols)]

    def low_slot(head):
        return wlow.at[z, head]

    def high_slot(head):
        return whigh.at[x, head - half_heads]

    sends = []
    kinds = ((tp < half_heads, low_piece, low_slot), (tp >= half_heads, high_piece, high_slot))

    def spread(finish):
        for mine_kind, part, slot in kinds:
            @pl.when(mine_kind)
            def _(part=part, slot=slot):
                kept_piece = pltpu.make_async_copy(part(core), slot(tp), local_sem.at[5])
                if finish:
                    kept_piece.wait()
                else:
                    kept_piece.start()
                for o in range(1, ntp):
                    to = lax.rem(tp + o, ntp)
                    copy = pltpu.make_async_remote_copy(
                        src_ref=part(lax.rem(to, CORES)), dst_ref=slot(tp),
                        send_sem=w_send.at[o], recv_sem=w_recv.at[tp],
                        device_id=(req, to), device_id_type=MESH,
                    )
                    if finish:
                        copy.wait_send()
                    else:
                        copy.start()

    spread(False)

    ring_y = Ring(ny, y, y_dev, lambda pos, h: nbuf.at[pos, core, h], y_send, y_recv)
    ring_y.own()

    def share(way, dist, h):
        owner = ring_y.place(way, dist) if dist else y
        copy = pltpu.make_async_remote_copy(
            src_ref=nbuf.at[owner, core, h],
            dst_ref=nbuf.at[owner, core, h],
            send_sem=p_send.at[way, dist, h],
            recv_sem=p_recv.at[way, dist, h],
            device_id=mate,
            device_id_type=MESH,
        )
        copy.start()
        sends.append(copy)

    def shared(way, dist, h):
        owner = ring_y.place(way, dist) if dist else y
        ref = nbuf.at[owner, 1 - core, h]
        pltpu.make_async_remote_copy(
            src_ref=ref, dst_ref=ref,
            send_sem=p_send.at[way, dist, h], recv_sem=p_recv.at[way, dist, h],
            device_id=mate, device_id_type=MESH,
        ).wait_recv()

    for h in range(2):
        share(0, 0, h)

    slope = jnp.exp2(jnp.full((1, HD), -8.0 / ntp, jnp.float32) * (tp + 1).astype(jnp.float32))[:, :1]
    scale = 1.0 / math.sqrt(HD)
    contract_last = (((1,), (1,)), ((), ()))

    def request(rid, q, k, v):
        length = lens[rid]
        mask = anc[rid]
        cells = kv.shape[2]
        depth = lax.dot_general(
            jnp.ones((8, drafts), jnp.bfloat16), mask.astype(jnp.float32).astype(jnp.bfloat16),
            contract_last, preferred_element_type=jnp.float32,
        )[:1] - 1.0
        cell = lax.broadcasted_iota(jnp.int32, (1, cells), 1)
        s_cache = lax.dot_general(q, kv[0, rid], contract_last, preferred_element_type=jnp.float32)
        s_cache = s_cache * scale + slope * cell.astype(jnp.float32)
        s_cache = jnp.where(cell < length, s_cache, -1e30)
        s_draft = lax.dot_general(q, k, contract_last, preferred_element_type=jnp.float32)
        s_draft = s_draft * scale + slope * (length.astype(jnp.float32) + depth)
        s_draft = jnp.where(mask == 1, s_draft, -1e30)
        top = jnp.maximum(jnp.max(s_cache, axis=1, keepdims=True), jnp.max(s_draft, axis=1, keepdims=True))
        e_cache = jnp.exp(s_cache - top)
        e_draft = jnp.exp(s_draft - top)
        total = jnp.sum(e_cache, axis=1, keepdims=True) + jnp.sum(e_draft, axis=1, keepdims=True)
        summed = jnp.dot(e_cache.astype(jnp.bfloat16), kv[1, rid], preferred_element_type=jnp.float32)
        summed += jnp.dot(e_draft.astype(jnp.bfloat16), v, preferred_element_type=jnp.float32)
        slots = kept.shape[2]
        slot = lax.broadcasted_iota(jnp.int32, (slots, drafts), 0)
        chosen = jnp.zeros((slots, drafts), jnp.int32)
        for a in range(slots):
            chosen = jnp.where(slot == a, accepted[a, rid], chosen)
        onehot = jnp.where(chosen == lax.broadcasted_iota(jnp.int32, (slots, drafts), 1), 1.0, 0.0).astype(jnp.bfloat16)
        kept[0, rid] = jnp.dot(onehot, k, preferred_element_type=jnp.float32).astype(jnp.bfloat16)
        kept[1, rid] = jnp.dot(onehot, v, preferred_element_type=jnp.float32).astype(jnp.bfloat16)
        return (summed / total).astype(jnp.bfloat16)

    order = []

    def attend(way, dist):
        if dist == 0:
            waits = [(0, 0, 0), (0, 0, 1)]
        elif dist < ring_y.far:
            waits = [(way, dist, 0), (way, dist, 1)]
        else:
            waits = [(0, dist, 0), (1, dist, 1)]
        for w in waits:
            shared(*w)
        owner = ring_y.place(way, dist) if dist else y
        tokens = nbuf[owner].reshape(CORES * drafts, width)
        joined = jnp.dot(tokens, wq[...], preferred_element_type=jnp.float32).astype(jnp.bfloat16)
        result = []
        for r in range(CORES):
            part = joined[r * drafts:(r + 1) * drafts]
            result.append(request(owner * CORES + r, part[:, :HD], part[:, HD:2 * HD], part[:, 2 * HD:]))
        result = jnp.concatenate(result, axis=0)
        if dist == 0:
            arecv[y, core] = result
            relay(0)
        else:
            offset = ny - dist if way == 0 else dist
            asend[offset] = result
            copy = pltpu.make_async_remote_copy(
                src_ref=asend.at[offset], dst_ref=arecv.at[y, core],
                send_sem=a_send.at[offset], recv_sem=a_recv.at[offset],
                device_id=y_dev(owner), device_id_type=MESH,
            )
            copy.start()
            sends.append(copy)
            order.append(offset)

    def source(offset):
        return lax.rem(y + ny - offset, ny) if offset else y

    def relay(offset):
        ref = arecv.at[source(offset), core]
        copy = pltpu.make_async_remote_copy(
            src_ref=ref, dst_ref=ref,
            send_sem=r_send.at[offset], recv_sem=r_recv.at[offset],
            device_id=mate, device_id_type=MESH,
        )
        copy.start()
        sends.append(copy)

    ring_z = Ring(nz, z, z_dev, lambda pos, h: wlow.at[pos, pl.ds(h * quarter, quarter)], z_send, z_recv)
    ring_x = Ring(nx, x, x_dev, lambda pos, h: whigh.at[pos, pl.ds(h * quarter, quarter)], x_send, x_recv)

    for load in loads:
        load.wait()
    attend(0, 0)

    spread(True)
    for head in range(ntp):
        @pl.when(tp != head)
        def _(head=head):
            ref = low_slot(head) if head < half_heads else high_slot(head)
            pltpu.make_async_remote_copy(
                src_ref=ref, dst_ref=ref, send_sem=w_send.at[0], recv_sem=w_recv.at[head],
                device_id=mate, device_id_type=MESH,
            ).wait_recv()
    ring_z.own()
    ring_x.own()

    along_z, along_x = ring_z.events(), ring_x.events()
    pending = []
    for i, event in enumerate(ring_y.events()):
        ring_y.event(event, share)
        if i:
            ring_z.event(along_z.pop(0))
        if i % 2 == 0 and i:
            ring_x.event(along_x.pop(0))
        dist, h = event
        if h == 1:
            pending += [(0, dist), (1, dist)]
        elif h is None:
            pending.insert(0, (0, dist))
        if pending:
            attend(*pending.pop(0))
    while pending or along_z or along_x:
        if along_z:
            ring_z.event(along_z.pop(0))
        if along_x:
            ring_x.event(along_x.pop(0))
        if pending:
            attend(*pending.pop(0))

    for offset in order:
        ref = arecv.at[source(offset), core]
        pltpu.make_async_remote_copy(
            src_ref=ref, dst_ref=ref, send_sem=a_send.at[offset], recv_sem=a_recv.at[offset],
            device_id=mate, device_id_type=MESH,
        ).wait_recv()
        relay(offset)

    for offset in [0] + order:
        ref = arecv.at[source(offset), 1 - core]
        pltpu.make_async_remote_copy(
            src_ref=ref, dst_ref=ref, send_sem=r_send.at[offset], recv_sem=r_recv.at[offset],
            device_id=mate, device_id_type=MESH,
        ).wait_recv()
    for chip in range(ny):
        left = jnp.concatenate([arecv[chip, c] for c in range(CORES)], axis=1)
        for b in range(nx):
            columns = pl.ds(b * piece_cols, piece_cols)
            right = []
            for head in range(chip * CORES, (chip + 1) * CORES):
                if head < half_heads:
                    right.append(wlow[:, head, :, columns].reshape(HD, piece_cols))
                else:
                    right.append(whigh[b, head - half_heads])
            term = jnp.dot(left, jnp.concatenate(right, axis=0), preferred_element_type=jnp.float32)
            acc[:, columns] = term if chip == 0 else acc[:, columns] + term

    for c in range(CORES):
        asend_rows = acc[c * drafts:(c + 1) * drafts].astype(jnp.bfloat16)
        obuf[c] = asend_rows
    last = pltpu.make_async_remote_copy(
        src_ref=obuf.at[1 - core], dst_ref=obuf.at[2], send_sem=o_send, recv_sem=o_recv,
        device_id=mate, device_id_type=MESH,
    )
    last.start()
    mine = pl.ds(pl.multiple_of(core * half_width, half_width), half_width)
    other = pl.ds(pl.multiple_of((1 - core) * half_width, half_width), half_width)
    out[:, mine] = obuf[core]
    last.wait()
    out[:, other] = obuf[2]
    for copy in sends:
        copy.wait_send()
    for ring in (ring_y, ring_z, ring_x):
        ring.drain()


def on_device(nz, req_size, tp_size, hidden, ln_gain, w_qkv, w_out, cache_kv, cache_len, ancestors, accepted):
    nx, ny = req_size // nz, tp_size // CORES
    drafts, width = hidden.shape
    requests, slots = accepted.shape
    half_width = width // CORES
    bf16 = jnp.bfloat16
    dma = pltpu.SemaphoreType.DMA
    vmem = pl.BlockSpec(memory_space=pltpu.VMEM)
    hbm = pl.BlockSpec(memory_space=pltpu.HBM)
    ring = lambda n: [dma((2, n // 2, 2))] * 2
    out, kept = pl.pallas_call(
        functools.partial(kernel, nx, nz, ny),
        out_shape=(
            jax.ShapeDtypeStruct((drafts, width), bf16),
            jax.ShapeDtypeStruct((2, requests, slots, HD), bf16),
        ),
        in_specs=[hbm] * 8,
        out_specs=(vmem, vmem),
        scratch_shapes=[
            pltpu.VMEM(hidden.shape, bf16),
            pltpu.VMEM((1, width), jnp.float32),
            pltpu.VMEM(w_out.shape, bf16),
            pltpu.SMEM(cache_len.shape, jnp.int32),
            pltpu.SMEM((slots, requests), jnp.int32),
            pltpu.VMEM((ny, CORES, 2, drafts // 2, width), bf16),
            pltpu.VMEM((nz, tp_size // 2, HD // nz, half_width), bf16),
            pltpu.VMEM((nx, tp_size // 2, HD, half_width // nx), bf16),
            pltpu.VMEM((width, 3 * HD), bf16),
            pltpu.VMEM(cache_kv.shape, bf16),
            pltpu.VMEM(ancestors.shape, jnp.int32),
            pltpu.VMEM((ny, CORES * drafts, HD), bf16),
            pltpu.VMEM((ny, CORES, CORES * drafts, HD), bf16),
            pltpu.VMEM((3, drafts, half_width), bf16),
            pltpu.VMEM((CORES * drafts, half_width), jnp.float32),
            dma((11,)),
            dma((tp_size,)),
            dma((tp_size,)),
            *ring(ny),
            dma((2, ny // 2 + 1, 2)),
            dma((2, ny // 2 + 1, 2)),
            *ring(nz), *ring(nx),
            dma((ny,)), dma((ny,)), dma((ny,)), dma((ny,)),
            dma, dma,
        ],
        compiler_params=pltpu.CompilerParams(
            collective_id=0, has_side_effects=True, vmem_limit_bytes=62 * 1024 * 1024
        ),
    )(
        hidden, ln_gain.reshape(1, width), w_out, cache_len, accepted.T,
        jnp.transpose(w_qkv, (1, 0, 2)), cache_kv, ancestors,
    )
    return (out, kept)


def solution(mesh, nz=8):
    placed = (
        P(("req", "tp"), None),
        P(),
        P(None, None, "tp"),
        P("tp", None),
        P(None, "req", None, "tp"),
        P("req"),
        P("req", None, None),
        P("req", None),
    )
    return jax.shard_map(
        functools.partial(on_device, nz, mesh.shape["req"], mesh.shape["tp"]),
        mesh=mesh,
        in_specs=placed,
        out_specs=(P(("req", "tp"), None), P(None, "req", None, "tp")),
        check_vma=False,
    )
```

```python
import functools
import math

import jax
import jax.numpy as jnp
from jax import lax
from jax.experimental import pallas as pl
from jax.experimental.pallas import tpu as pltpu
from jax.sharding import PartitionSpec as P

HD = 128
CORES = 2
MESH = pl.DeviceIdType.MESH


class Ring:
    def __init__(self, n, me, device, slot, send, recv):
        self.n, self.me, self.device, self.slot = n, me, device, slot
        self.send, self.recv = send, recv
        self.far = n // 2
        self.sent = []

    def live(self, way, dist, h):
        return dist < self.far or (dist == self.far and h == way)

    def place(self, way, dist):
        step = self.n - dist if way == 0 else dist
        return lax.rem(self.me + step, self.n)

    def copy(self, way, dist, h):
        owner = self.me if dist == 1 else self.place(way, dist - 1)
        to = lax.rem(self.me + (1 if way == 0 else self.n - 1), self.n)
        ref = self.slot(owner, h)
        return pltpu.make_async_remote_copy(
            src_ref=ref,
            dst_ref=ref,
            send_sem=self.send.at[way, dist - 1, h],
            recv_sem=self.recv.at[way, dist - 1, h],
            device_id=self.device(to),
            device_id_type=MESH,
        )

    def start(self, way, dist, h):
        if self.live(way, dist, h):
            copy = self.copy(way, dist, h)
            copy.start()
            self.sent.append(copy)

    def own(self):
        for h in range(2):
            for way in range(2):
                self.start(way, 1, h)

    def step(self, dist, h, then=None):
        for way in range(2):
            if self.live(way, dist, h):
                ref = self.slot(self.place(way, dist), h)
                pltpu.make_async_remote_copy(
                    src_ref=ref,
                    dst_ref=ref,
                    send_sem=self.send.at[way, dist - 1, h],
                    recv_sem=self.recv.at[way, dist - 1, h],
                    device_id=self.device(lax.rem(self.me + 1, self.n)),
                    device_id_type=MESH,
                ).wait_recv()
                self.start(way, dist + 1, h)
                if then is not None:
                    then(way, dist, h)

    def events(self):
        return [(d, h) for d in range(1, self.far) for h in range(2)] + [(self.far, None)]

    def event(self, event, then=None):
        dist, h = event
        for half in (0, 1) if h is None else (h,):
            self.step(dist, half, then)

    def drain(self):
        for copy in self.sent:
            copy.wait_send()


def kernel(
    nx, nz, ny,
    hidden_hbm, gain_hbm, w_out_hbm, lens_hbm, accepted_hbm, w_qkv, cache, ancestors,
    out, kept,
    hidden, gain, w_out, lens, accepted, nbuf, wlow, whigh, wq, kv, anc, asend, arecv, obuf, acc,
    local_sem, w_send, w_recv,
    y_send, y_recv, p_send, p_recv,
    z_send, z_recv, x_send, x_recv,
    a_send, a_recv, r_send, r_recv, o_send, o_recv,
):
    req, tp = lax.axis_index("req"), lax.axis_index("tp")
    x, z = lax.div(req, nz), lax.rem(req, nz)
    y, core = lax.div(tp, CORES), lax.rem(tp, CORES)
    ntp = ny * CORES
    half_heads = ntp // 2
    quarter = ntp // 4
    mate = (req, y * CORES + (1 - core))
    drafts, width = hidden.shape
    half_rows = drafts // 2
    half_width = width // CORES
    piece_rows, piece_cols = HD // nz, half_width // nx

    barrier = pltpu.get_barrier_semaphore()
    x_dev = lambda pos: (pos * nz + z, tp)
    z_dev = lambda pos: (x * nz + pos, tp)
    y_dev = lambda pos: (req, pos * CORES + core)
    peers = [(req, lax.rem(tp + o, ntp)) for o in range(1, ntp)]
    peers += [x_dev(lax.rem(x + s, nx)) for s in (1, nx - 1)]
    peers += [z_dev(lax.rem(z + s, nz)) for s in (1, nz - 1)]
    early = [
        pltpu.make_async_copy(src, dst, local_sem.at[6 + i])
        for i, (src, dst) in enumerate(((hidden_hbm, hidden), (gain_hbm, gain), (w_out_hbm, w_out)))
    ]
    for load in early:
        load.start()
    for peer in peers:
        pl.semaphore_signal(barrier, inc=1, device_id=peer, device_id_type=MESH)

    loads = [pltpu.make_async_copy(w_qkv.at[i], wq.at[:, pl.ds(i * HD, HD)], local_sem.at[i]) for i in range(3)]
    loads.append(pltpu.make_async_copy(cache, kv, local_sem.at[3]))
    loads.append(pltpu.make_async_copy(ancestors, anc, local_sem.at[4]))
    loads.append(pltpu.make_async_copy(lens_hbm, lens, local_sem.at[9]))
    loads.append(pltpu.make_async_copy(accepted_hbm, accepted, local_sem.at[10]))
    for load in loads:
        load.start()

    early[0].wait()
    early[1].wait()
    rows = hidden[...].astype(jnp.float32)
    mean = jnp.mean(rows, axis=1, keepdims=True)
    centered = rows - mean
    var = jnp.mean(centered * centered, axis=1, keepdims=True)
    normed = (centered * lax.rsqrt(var + 1e-05) * gain[...]).astype(jnp.bfloat16)
    nbuf[y, core, 0] = normed[:half_rows]
    nbuf[y, core, 1] = normed[half_rows:]

    early[2].wait()
    pl.semaphore_wait(barrier, len(peers))

    def low_piece(c):
        return w_out.at[
            pl.ds(pl.multiple_of(z * piece_rows, piece_rows), piece_rows),
            pl.ds(pl.multiple_of(c * half_width, half_width), half_width),
        ]

    def high_piece(c):
        return w_out.at[:, pl.ds(pl.multiple_of(c * half_width + x * piece_cols, piece_cols), piece_cols)]

    def low_slot(head):
        return wlow.at[z, head]

    def high_slot(head):
        return whigh.at[x, head - half_heads]

    sends = []
    kinds = ((tp < half_heads, low_piece, low_slot), (tp >= half_heads, high_piece, high_slot))

    def spread(finish):
        for mine_kind, part, slot in kinds:
            @pl.when(mine_kind)
            def _(part=part, slot=slot):
                kept_piece = pltpu.make_async_copy(part(core), slot(tp), local_sem.at[5])
                if finish:
                    kept_piece.wait()
                else:
                    kept_piece.start()
                for o in range(1, ntp):
                    to = lax.rem(tp + o, ntp)
                    copy = pltpu.make_async_remote_copy(
                        src_ref=part(lax.rem(to, CORES)), dst_ref=slot(tp),
                        send_sem=w_send.at[o], recv_sem=w_recv.at[tp],
                        device_id=(req, to), device_id_type=MESH,
                    )
                    if finish:
                        copy.wait_send()
                    else:
                        copy.start()

    spread(False)

    ring_y = Ring(ny, y, y_dev, lambda pos, h: nbuf.at[pos, core, h], y_send, y_recv)
    ring_y.own()

    def share(way, dist, h):
        owner = ring_y.place(way, dist) if dist else y
        copy = pltpu.make_async_remote_copy(
            src_ref=nbuf.at[owner, core, h],
            dst_ref=nbuf.at[owner, core, h],
            send_sem=p_send.at[way, dist, h],
            recv_sem=p_recv.at[way, dist, h],
            device_id=mate,
            device_id_type=MESH,
        )
        copy.start()
        sends.append(copy)

    def shared(way, dist, h):
        owner = ring_y.place(way, dist) if dist else y
        ref = nbuf.at[owner, 1 - core, h]
        pltpu.make_async_remote_copy(
            src_ref=ref, dst_ref=ref,
            send_sem=p_send.at[way, dist, h], recv_sem=p_recv.at[way, dist, h],
            device_id=mate, device_id_type=MESH,
        ).wait_recv()

    for h in range(2):
        share(0, 0, h)

    slope = jnp.exp2(jnp.full((1, HD), -8.0 / ntp, jnp.float32) * (tp + 1).astype(jnp.float32))[:, :1]
    scale = 1.0 / math.sqrt(HD)
    contract_last = (((1,), (1,)), ((), ()))

    def request(rid, q, k, v):
        length = lens[rid]
        mask = anc[rid]
        cells = kv.shape[2]
        depth = lax.dot_general(
            jnp.ones((8, drafts), jnp.bfloat16), mask.astype(jnp.float32).astype(jnp.bfloat16),
            contract_last, preferred_element_type=jnp.float32,
        )[:1] - 1.0
        cell = lax.broadcasted_iota(jnp.int32, (1, cells), 1)
        s_cache = lax.dot_general(q, kv[0, rid], contract_last, preferred_element_type=jnp.float32)
        s_cache = s_cache * scale + slope * cell.astype(jnp.float32)
        s_cache = jnp.where(cell < length, s_cache, -1e30)
        s_draft = lax.dot_general(q, k, contract_last, preferred_element_type=jnp.float32)
        s_draft = s_draft * scale + slope * (length.astype(jnp.float32) + depth)
        s_draft = jnp.where(mask == 1, s_draft, -1e30)
        top = jnp.maximum(jnp.max(s_cache, axis=1, keepdims=True), jnp.max(s_draft, axis=1, keepdims=True))
        e_cache = jnp.exp(s_cache - top)
        e_draft = jnp.exp(s_draft - top)
        total = jnp.sum(e_cache, axis=1, keepdims=True) + jnp.sum(e_draft, axis=1, keepdims=True)
        summed = jnp.dot(e_cache.astype(jnp.bfloat16), kv[1, rid], preferred_element_type=jnp.float32)
        summed += jnp.dot(e_draft.astype(jnp.bfloat16), v, preferred_element_type=jnp.float32)
        slots = kept.shape[2]
        slot = lax.broadcasted_iota(jnp.int32, (slots, drafts), 0)
        chosen = jnp.zeros((slots, drafts), jnp.int32)
        for a in range(slots):
            chosen = jnp.where(slot == a, accepted[a, rid], chosen)
        onehot = jnp.where(chosen == lax.broadcasted_iota(jnp.int32, (slots, drafts), 1), 1.0, 0.0).astype(jnp.bfloat16)
        kept[0, rid] = jnp.dot(onehot, k, preferred_element_type=jnp.float32).astype(jnp.bfloat16)
        kept[1, rid] = jnp.dot(onehot, v, preferred_element_type=jnp.float32).astype(jnp.bfloat16)
        return (summed / total).astype(jnp.bfloat16)

    order = []

    def attend(way, dist):
        if dist == 0:
            waits = [(0, 0, 0), (0, 0, 1)]
        elif dist < ring_y.far:
            waits = [(way, dist, 0), (way, dist, 1)]
        else:
            waits = [(0, dist, 0), (1, dist, 1)]
        for w in waits:
            shared(*w)
        owner = ring_y.place(way, dist) if dist else y
        tokens = nbuf[owner].reshape(CORES * drafts, width)
        joined = jnp.dot(tokens, wq[...], preferred_element_type=jnp.float32).astype(jnp.bfloat16)
        result = []
        for r in range(CORES):
            part = joined[r * drafts:(r + 1) * drafts]
            result.append(request(owner * CORES + r, part[:, :HD], part[:, HD:2 * HD], part[:, 2 * HD:]))
        result = jnp.concatenate(result, axis=0)
        if dist == 0:
            arecv[y, core] = result
            relay(0)
        else:
            offset = ny - dist if way == 0 else dist
            asend[offset] = result
            copy = pltpu.make_async_remote_copy(
                src_ref=asend.at[offset], dst_ref=arecv.at[y, core],
                send_sem=a_send.at[offset], recv_sem=a_recv.at[offset],
                device_id=y_dev(owner), device_id_type=MESH,
            )
            copy.start()
            sends.append(copy)
            order.append(offset)
            if dist == ring_y.far:
                copy = pltpu.make_async_remote_copy(
                    src_ref=asend.at[offset], dst_ref=arecv.at[y, core],
                    send_sem=r_send.at[offset], recv_sem=r_recv.at[offset],
                    device_id=(req, owner * CORES + 1 - core), device_id_type=MESH,
                )
                copy.start()
                sends.append(copy)

    def source(offset):
        return lax.rem(y + ny - offset, ny) if offset else y

    def relay(offset):
        ref = arecv.at[source(offset), core]
        copy = pltpu.make_async_remote_copy(
            src_ref=ref, dst_ref=ref,
            send_sem=r_send.at[offset], recv_sem=r_recv.at[offset],
            device_id=mate, device_id_type=MESH,
        )
        copy.start()
        sends.append(copy)

    ring_z = Ring(nz, z, z_dev, lambda pos, h: wlow.at[pos, pl.ds(h * quarter, quarter)], z_send, z_recv)
    ring_x = Ring(nx, x, x_dev, lambda pos, h: whigh.at[pos, pl.ds(h * quarter, quarter)], x_send, x_recv)

    for load in loads:
        load.wait()
    attend(0, 0)

    spread(True)
    for head in range(ntp):
        @pl.when(tp != head)
        def _(head=head):
            ref = low_slot(head) if head < half_heads else high_slot(head)
            pltpu.make_async_remote_copy(
                src_ref=ref, dst_ref=ref, send_sem=w_send.at[0], recv_sem=w_recv.at[head],
                device_id=mate, device_id_type=MESH,
            ).wait_recv()
    ring_z.own()
    ring_x.own()

    along_z, along_x = ring_z.events(), ring_x.events()
    pending = []
    for i, event in enumerate(ring_y.events()):
        ring_y.event(event, share)
        if i:
            ring_z.event(along_z.pop(0))
        if i % 2 == 0 and i:
            ring_x.event(along_x.pop(0))
        dist, h = event
        if h == 1:
            pending += [(0, dist), (1, dist)]
        elif h is None:
            pending.insert(0, (0, dist))
        if pending:
            attend(*pending.pop(0))
        if pending and dist == ring_y.far - 1 and h == 1:
            attend(*pending.pop(0))
    while pending or along_z or along_x:
        if along_z:
            ring_z.event(along_z.pop(0))
        if along_x:
            ring_x.event(along_x.pop(0))
        if pending:
            attend(*pending.pop(0))

    for offset in sorted(order, key=lambda o: o == ring_y.far):
        ref = arecv.at[source(offset), core]
        pltpu.make_async_remote_copy(
            src_ref=ref, dst_ref=ref, send_sem=a_send.at[offset], recv_sem=a_recv.at[offset],
            device_id=mate, device_id_type=MESH,
        ).wait_recv()
        if offset != ring_y.far:
            relay(offset)

    for offset in [0] + order:
        ref = arecv.at[source(offset), 1 - core]
        pltpu.make_async_remote_copy(
            src_ref=ref, dst_ref=ref, send_sem=r_send.at[offset], recv_sem=r_recv.at[offset],
            device_id=mate, device_id_type=MESH,
        ).wait_recv()
    for chip in range(ny):
        left = jnp.concatenate([arecv[chip, c] for c in range(CORES)], axis=1)
        for b in range(nx):
            columns = pl.ds(b * piece_cols, piece_cols)
            right = []
            for head in range(chip * CORES, (chip + 1) * CORES):
                if head < half_heads:
                    right.append(wlow[:, head, :, columns].reshape(HD, piece_cols))
                else:
                    right.append(whigh[b, head - half_heads])
            term = jnp.dot(left, jnp.concatenate(right, axis=0), preferred_element_type=jnp.float32)
            acc[:, columns] = term if chip == 0 else acc[:, columns] + term

    for c in range(CORES):
        asend_rows = acc[c * drafts:(c + 1) * drafts].astype(jnp.bfloat16)
        obuf[c] = asend_rows
    last = pltpu.make_async_remote_copy(
        src_ref=obuf.at[1 - core], dst_ref=obuf.at[2], send_sem=o_send, recv_sem=o_recv,
        device_id=mate, device_id_type=MESH,
    )
    last.start()
    mine = pl.ds(pl.multiple_of(core * half_width, half_width), half_width)
    other = pl.ds(pl.multiple_of((1 - core) * half_width, half_width), half_width)
    out[:, mine] = obuf[core]
    last.wait()
    out[:, other] = obuf[2]
    for copy in sends:
        copy.wait_send()
    for ring in (ring_y, ring_z, ring_x):
        ring.drain()


def on_device(nz, req_size, tp_size, hidden, ln_gain, w_qkv, w_out, cache_kv, cache_len, ancestors, accepted):
    nx, ny = req_size // nz, tp_size // CORES
    drafts, width = hidden.shape
    requests, slots = accepted.shape
    half_width = width // CORES
    bf16 = jnp.bfloat16
    dma = pltpu.SemaphoreType.DMA
    vmem = pl.BlockSpec(memory_space=pltpu.VMEM)
    hbm = pl.BlockSpec(memory_space=pltpu.HBM)
    ring = lambda n: [dma((2, n // 2, 2))] * 2
    out, kept = pl.pallas_call(
        functools.partial(kernel, nx, nz, ny),
        out_shape=(
            jax.ShapeDtypeStruct((drafts, width), bf16),
            jax.ShapeDtypeStruct((2, requests, slots, HD), bf16),
        ),
        in_specs=[hbm] * 8,
        out_specs=(vmem, vmem),
        scratch_shapes=[
            pltpu.VMEM(hidden.shape, bf16),
            pltpu.VMEM((1, width), jnp.float32),
            pltpu.VMEM(w_out.shape, bf16),
            pltpu.SMEM(cache_len.shape, jnp.int32),
            pltpu.SMEM((slots, requests), jnp.int32),
            pltpu.VMEM((ny, CORES, 2, drafts // 2, width), bf16),
            pltpu.VMEM((nz, tp_size // 2, HD // nz, half_width), bf16),
            pltpu.VMEM((nx, tp_size // 2, HD, half_width // nx), bf16),
            pltpu.VMEM((width, 3 * HD), bf16),
            pltpu.VMEM(cache_kv.shape, bf16),
            pltpu.VMEM(ancestors.shape, jnp.int32),
            pltpu.VMEM((ny, CORES * drafts, HD), bf16),
            pltpu.VMEM((ny, CORES, CORES * drafts, HD), bf16),
            pltpu.VMEM((3, drafts, half_width), bf16),
            pltpu.VMEM((CORES * drafts, half_width), jnp.float32),
            dma((11,)),
            dma((tp_size,)),
            dma((tp_size,)),
            *ring(ny),
            dma((2, ny // 2 + 1, 2)),
            dma((2, ny // 2 + 1, 2)),
            *ring(nz), *ring(nx),
            dma((ny,)), dma((ny,)), dma((ny,)), dma((ny,)),
            dma, dma,
        ],
        compiler_params=pltpu.CompilerParams(
            collective_id=0, has_side_effects=True, vmem_limit_bytes=62 * 1024 * 1024
        ),
    )(
        hidden, ln_gain.reshape(1, width), w_out, cache_len, accepted.T,
        jnp.transpose(w_qkv, (1, 0, 2)), cache_kv, ancestors,
    )
    return (out, kept)


def solution(mesh, nz=8):
    placed = (
        P(("req", "tp"), None),
        P(),
        P(None, None, "tp"),
        P("tp", None),
        P(None, "req", None, "tp"),
        P("req"),
        P("req", None, None),
        P("req", None),
    )
    return jax.shard_map(
        functools.partial(on_device, nz, mesh.shape["req"], mesh.shape["tp"]),
        mesh=mesh,
        in_specs=placed,
        out_specs=(P(("req", "tp"), None), P(None, "req", None, "tp")),
        check_vma=False,
    )
```
